128 devices in a mesh: dom: 4 (over x), tile: 32 (over y, z, core).
Axes of the slice: x: 4, y: 4, z: 4, core: 2. Of those that a mesh axis runs over, the one named last changes fastest.
Arguments:
- atm_anom: bfloat16 [512, 80, 127, 128], P(('dom', 'tile')), may hold values from -0.25 to 0.25
- ocn_anom: bfloat16 [512, 80, 75, 128], P(('dom', 'tile')), may hold values from -0.25 to 0.25
- atm_vec: bfloat16 [512, 127, 128], P(('dom', 'tile')), may hold values from -6 to 6
- ocn_vec: bfloat16 [512, 75, 128], P(('dom', 'tile')), may hold values from -6 to 6
- atm_to_ocean: int32 [512, 128], P(('dom', 'tile')), may hold values from 0 to 65535, as said below
- sea_tiles: int32 [512], P(('dom', 'tile')), may hold values 0 or 1
- atm_class: int32 [512, 5], P(('dom', 'tile')), may hold values from 0 to 4
- ocn_class: int32 [512, 5], P(('dom', 'tile')), may hold values from 0 to 4
Outputs:
- atm_out: float32 [512, 127, 128], P(('dom', 'tile'))
- ocn_out: float32 [512, 75, 128], P(('dom', 'tile'))
The draws below stay inside these ranges and needn't reach their ends.
Inputs may be any that keep to these rules, and one draw needn't show every extreme that they name: atm_to_ocean is one to one onto all 65536 ocean columns; the atmosphere columns held by the r-th device along dom+tile (tiles r * 4 to r * 4 + 3) are paired exactly with the ocean columns whose column index c satisfies c // (128 / number of devices) = r.
All inputs are finite; a program needn't handle non-finite values. No bound on the sum of `sea_tiles` on one device may be relied on, other than what follows from the above.
Results may differ from the reference program's by a relative error of at most 0.0029.
Values may be sent and summed in bfloat16 or wider, within the bound.
A program may use at most 64 MiB of HBM per device.

```python
import jax
import jax.numpy as jnp
from jax import lax

M = 80
LA = 127
LO = 75
C = 128
KA = 16
KO = 16
HALO = 2
TILE_DEV = 4
TILES = 512
N_DOM = 4
N_TILE = 32


def draw_atm_to_ocean(key, part):
    device_count = N_DOM * N_TILE
    per_peer = C // device_count
    slot_count = TILE_DEV * C

    def one_sender(sender):
        shuffled = jax.random.permutation(jax.random.fold_in(key, sender), slot_count).astype(jnp.int32)
        dest_local = shuffled // C
        position = shuffled % C
        dest_device = position // per_peer
        column = sender * per_peer + position % per_peer
        return ((dest_device * TILE_DEV + dest_local) * C + column).astype(jnp.int32)
    paired = jax.vmap(one_sender)(jnp.arange(device_count, dtype=jnp.int32))
    return paired.reshape(TILES, C)


def with_ends(drawn, own_key, smallest, high):
    dims = drawn.shape
    spot = [jax.random.randint(jax.random.fold_in(own_key, axis), (), 0, dims[axis]) for axis in range(len(dims))]
    drawn = drawn.at[tuple(spot)].set(smallest)
    longest = dims.index(max(dims))
    spot[longest] = (spot[longest] + 1) % dims[longest]
    return drawn.at[tuple(spot)].set(high)


def shard_levels(own_key, dims, pieces, least, high):
    factor_of = 1.0
    for axis_at, parts in pieces:
        draws = jax.random.uniform(jax.random.fold_in(jax.random.fold_in(own_key, 6), axis_at), (parts,), jnp.float32, least / len(pieces), high / len(pieces))
        factor_of = factor_of * jnp.repeat(jnp.exp(draws), dims[axis_at] // parts).reshape((-1,) + (1,) * (len(dims) - 1 - axis_at))
    return factor_of


def scatter_about(own_key, dims, scale, reach, pieces=(), kind=jnp.bfloat16):
    entries = jax.random.normal(own_key, dims, jnp.float32) * scale
    if len(pieces) > 0:
        entries = shard_levels(own_key, dims, pieces, -0.22, 0.18) * entries
    return jnp.clip(entries, min=-reach, max=reach).astype(kind)


def setup_inputs(seed: int = 0) -> dict:
    seeds = jax.random.split(jax.random.key(seed), 9)
    atm_anom = scatter_about(seeds[0], (TILES, M, LA, C), 0.04, 0.25, ((0, 128),))
    ocn_anom = scatter_about(seeds[1], (TILES, M, LO, C), 0.04, 0.25, ((0, 128),))
    atm_vec = scatter_about(seeds[2], (TILES, LA, C), 1.0, 6.0, ((0, 128),))
    ocn_vec = scatter_about(seeds[3], (TILES, LO, C), 1.0, 6.0, ((0, 128),))
    atm_to_ocean = draw_atm_to_ocean(jax.random.fold_in(seeds[8], 71), 0)
    sea_tiles = with_ends((jax.random.randint(seeds[5], (TILES,), 0, 4) < 3).astype(jnp.int32), jax.random.fold_in(seeds[5], 1), 0, 1)
    atm_class = with_ends(jax.random.randint(seeds[6], (TILES, 2 * HALO + 1), 0, 5), jax.random.fold_in(seeds[6], 1), 0, 4).astype(jnp.int32)
    ocn_class = with_ends(jax.random.randint(seeds[7], (TILES, 2 * HALO + 1), 0, 5), jax.random.fold_in(seeds[7], 1), 0, 4).astype(jnp.int32)
    return dict(atm_anom=atm_anom, ocn_anom=ocn_anom, atm_vec=atm_vec, ocn_vec=ocn_vec, atm_to_ocean=atm_to_ocean, sea_tiles=sea_tiles, atm_class=atm_class, ocn_class=ocn_class)


COUPLING = 8.0
ATM_SPREAD = 12.0
OCN_SPREAD = 8.0
CLASS_TABLE = (1.0, 0.7, 0.45, 0.25, 0.0)


def level_taper(level_count, spread):
    position = jnp.arange(level_count, dtype=jnp.float32)
    scaled = (position[:, None] - position[None, :]) / spread
    return jnp.exp(-0.5 * scaled * scaled)


def class_weights(classes):
    class_table = jnp.array(CLASS_TABLE, jnp.float32)
    matches = classes[..., None] == jnp.arange(len(CLASS_TABLE), dtype=jnp.int32)
    return jnp.sum(jnp.where(matches, class_table, 0.0), axis=-1)


def horizontal(coefficients, classes):
    weights = class_weights(classes)
    band_view = coefficients.reshape((N_DOM, N_TILE * TILE_DEV) + coefficients.shape[1:])
    summed = jnp.zeros_like(coefficients)
    for offset in range(-HALO, HALO + 1):
        rolled = jnp.roll(band_view, -offset, axis=1).reshape(coefficients.shape)
        summed = summed + weights[:, offset + HALO, None, None] * rolled
    return summed


def intra_apply(anomaly, vector, classes, tapering):
    coefficients = lax.map(lambda tile_pair: jnp.einsum("mlc,lc->ml", tile_pair[0].astype(jnp.float32), tile_pair[1].astype(jnp.float32)), (anomaly, vector))
    spread = horizontal(coefficients, classes)
    vertical_coeff = jnp.einsum("tmk,lk->tml", spread, tapering, precision=lax.Precision.HIGHEST).astype(jnp.bfloat16)
    return lax.map(lambda tile_pair: jnp.einsum("mlc,ml->lc", tile_pair[0].astype(jnp.float32), tile_pair[1].astype(jnp.float32)), (anomaly, vertical_coeff))


def reference(atm_anom, ocn_anom, atm_vec, ocn_vec, atm_to_ocean, sea_tiles, atm_class, ocn_class):
    ocean = ocn_anom * sea_tiles.astype(jnp.bfloat16)[:, None, None, None]
    atm_inc = intra_apply(atm_anom, atm_vec, atm_class, level_taper(LA, ATM_SPREAD))
    ocn_inc = intra_apply(ocean, ocn_vec, ocn_class, level_taper(LO, OCN_SPREAD))
    rise_position = jnp.arange(KA, dtype=jnp.float32)
    rise_weights = jnp.exp(-2.0 * (KA - 1 - rise_position) / KA)
    fall_position = jnp.arange(KO, dtype=jnp.float32)
    fall_weights = jnp.exp(-2.0 * fall_position / KO)
    atm_surface = atm_anom[:, :, LA - KA:, :].astype(jnp.float32)
    ocn_top = ocean[:, :, :KO, :].astype(jnp.float32)
    atm_weighted = atm_vec[:, LA - KA:, :].astype(jnp.float32) * rise_weights[None, :, None]
    ocn_weighted = ocn_vec[:, :KO, :].astype(jnp.float32) * fall_weights[None, :, None]
    atm_proj = jnp.einsum("tmsc,tsc->mtc", atm_surface, atm_weighted).astype(jnp.bfloat16)
    ocn_proj = jnp.einsum("tmoc,toc->mtc", ocn_top, ocn_weighted).astype(jnp.bfloat16)
    flat_width = TILES * C
    pairing = atm_to_ocean.reshape(flat_width).astype(jnp.int32)
    ocean_pair = jnp.zeros((M, flat_width), jnp.bfloat16).at[:, pairing].set(atm_proj.reshape(M, flat_width)).reshape(M, TILES, C)
    atm_pair = ocn_proj.reshape(M, flat_width)[:, pairing].reshape(M, TILES, C)
    atm_cross = COUPLING * rise_weights[None, :, None] * jnp.einsum("tmsc,mtc->tsc", atm_surface, atm_pair.astype(jnp.float32))
    ocn_cross = COUPLING * fall_weights[None, :, None] * jnp.einsum("tmoc,mtc->toc", ocn_top, ocean_pair.astype(jnp.float32))
    atm_out = atm_inc.at[:, LA - KA:, :].add(atm_cross)
    ocn_out = ocn_inc.at[:, :KO, :].add(ocn_cross)
    return (atm_out, ocn_out)
```

```python
import functools

import jax
import jax.numpy as jnp
import numpy as np
from jax import lax
from jax.experimental import pallas as pl
from jax.experimental.pallas import tpu as pltpu
from jax.sharding import PartitionSpec as P

M = 80
LA = 127
LO = 75
C = 128
KA = 16
KO = 16
TD = 4
BLOCK = 16
SURF = LA - KA
ROWS_A = 128
ROWS_O = 80
HALO_ROWS = ROWS_A + ROWS_O
PEERS = 128
PER_PEER = 8
ROUTE = PEERS * PER_PEER

COUPLING = 8.0
CLASS_TABLE = (1.0, 0.7, 0.45, 0.25, 0.0)
RISE = [float(np.exp(np.float32(-2.0 * (KA - 1 - s) / KA))) for s in range(KA)]
FALL = [float(np.exp(np.float32(-2.0 * o / KO))) for o in range(KO)]

F32 = jnp.float32
BF16 = jnp.bfloat16
MESH = pl.DeviceIdType.MESH


def class_weight(code):
    weight = jnp.float32(CLASS_TABLE[-1])
    for index in range(len(CLASS_TABLE) - 1):
        weight = jnp.where(code == index, jnp.float32(CLASS_TABLE[index]), weight)
    return weight


def taper_split(rows, levels, spread):
    row = lax.broadcasted_iota(jnp.int32, (rows, rows), 0)
    col = lax.broadcasted_iota(jnp.int32, (rows, rows), 1)
    scaled = (row - col).astype(F32) / spread
    full = jnp.exp(-0.5 * scaled * scaled)
    full = jnp.where((row < levels) & (col < levels), full, 0.0)
    high = full.astype(BF16)
    low = (full - high.astype(F32)).astype(BF16)
    return high, low


def dot(a, b):
    return lax.dot_general(a, b, (((1,), (0,)), ((), ())), preferred_element_type=F32)


def dot_nt(a, b):
    return lax.dot_general(a, b, (((1,), (1,)), ((), ())), preferred_element_type=F32)


def dot_tn(a, b):
    return lax.dot_general(a, b, (((0,), (0,)), ((), ())), preferred_element_type=F32)


def peer_of(step, me_dom, me_tile):
    def reach(k):
        return jnp.where(k < 2, k + 2, 3 - k)

    y, z, core = me_tile // 8, (me_tile // 2) % 4, me_tile % 2
    dom = (me_dom + reach(step // 32)) % 4
    y = (y + reach((step // 8) % 4)) % 4
    z = (z + reach((step // 2) % 4)) % 4
    core = (core + 1 - step % 2) % 2
    return dom, (y * 4 + z) * 2 + core


def kernel(
    atm_hbm, ocn_hbm, avec_hbm, ovec_hbm, pair_hbm, sea, acls, ocls, aout, oout,
    atm, ocn, avec, ovec, pairing, avf, ovf, send_map, recv_map, proj, outgoing, incoming,
    coeff_a, coeff_o, vert_a, vert_o, halo_out, halo_in, paired,
    load_sems, small_sems, send_sem, recv_sem, own_sem, halo_send, halo_recv,
):
    me_dom, me_tile = lax.axis_index("dom"), lax.axis_index("tile")
    me = me_dom * 32 + me_tile

    def small_loads():
        return [
            pltpu.make_async_copy(avec_hbm, avec, small_sems.at[0]),
            pltpu.make_async_copy(ovec_hbm, ovec, small_sems.at[1]),
            pltpu.make_async_copy(pair_hbm, pairing, small_sems.at[2]),
        ]

    def surface_loads():
        return [
            pltpu.make_async_copy(
                ocn_hbm.at[:, pl.ds(0, KO)], ocn.at[:, pl.ds(0, KO)], load_sems.at[0]
            ),
            pltpu.make_async_copy(
                atm_hbm.at[:, pl.ds(SURF, KA)], atm.at[:, pl.ds(SURF, KA)], load_sems.at[1]
            ),
        ]

    def tile_loads(t):
        return [
            pltpu.make_async_copy(
                atm_hbm.at[t, pl.ds(0, SURF)], atm.at[t, pl.ds(0, SURF)], load_sems.at[2 + 2 * t]
            ),
            pltpu.make_async_copy(
                ocn_hbm.at[t, pl.ds(KO, LO - KO)],
                ocn.at[t, pl.ds(KO, LO - KO)],
                load_sems.at[3 + 2 * t],
            ),
        ]

    for copy in small_loads() + surface_loads():
        copy.start()
    for t in range(TD):
        for copy in tile_loads(t):
            copy.start()

    barrier = pltpu.get_barrier_semaphore()

    def greet(step, carry):
        dom, tile = peer_of(step, me_dom, me_tile)
        pl.semaphore_signal(barrier, inc=1, device_id=(dom, tile), device_id_type=MESH)
        return carry

    lax.fori_loop(0, PEERS - 1, greet, 0)

    coeff_a[...] = jnp.zeros_like(coeff_a)
    coeff_o[...] = jnp.zeros_like(coeff_o)
    proj[pl.ds(M, C - M), :] = jnp.zeros((C - M, 2 * TD * C), BF16)

    for copy in small_loads():
        copy.wait()
    avf[...] = avec[...].astype(F32)
    ovf[...] = ovec[...].astype(F32)

    lane = lax.broadcasted_iota(jnp.int32, (1, C), 1)

    def build_maps(b, carry):
        start = pl.multiple_of(b * C, C)
        row = lax.broadcasted_iota(jnp.int32, (C, C), 0) + start
        for t in range(TD):
            slot = lax.shift_right_logical(pairing[pl.ds(t, 1), :], 7)
            spot = lax.shift_right_logical(slot, 2) * PER_PEER + (slot & 3)
            cols = pl.ds(t * C, C)
            send_map[pl.ds(start, C), cols] = jnp.where(row == spot, 1.0, 0.0).astype(BF16)
            recv_map[pl.ds(start, C), cols] = jnp.where(row == spot + 4, 1.0, 0.0).astype(BF16)
            cols = pl.ds((TD + t) * C, C)
            spot = lane * PER_PEER + t
            send_map[pl.ds(start, C), cols] = jnp.where(row == spot + 4, 1.0, 0.0).astype(BF16)
            recv_map[pl.ds(start, C), cols] = jnp.where(row == spot, 1.0, 0.0).astype(BF16)
        return carry

    lax.fori_loop(0, ROUTE // C, build_maps, 0)

    for copy in surface_loads():
        copy.wait()
    for t in range(TD):
        total = jnp.zeros((M, C), F32)
        for o in range(KO):
            row = ovf[o, pl.ds(t, 1), :] * FALL[o]
            total = total + ocn[t, o].astype(F32) * row
        wet = sea[t].astype(F32)
        proj[pl.ds(0, M), pl.ds((TD + t) * C, C)] = (total * wet).astype(BF16)
        total = jnp.zeros((M, C), F32)
        for s in range(KA):
            row = avf[SURF + s, pl.ds(t, 1), :] * RISE[s]
            total = total + atm[t, SURF + s].astype(F32) * row
        proj[pl.ds(0, M), pl.ds(t * C, C)] = total.astype(BF16)

    def fill_outgoing(b, carry):
        rows = dot_nt(send_map[pl.ds(pl.multiple_of(b * C, C), C), :], proj[...])
        outgoing[pl.ds(b * (C // PER_PEER), C // PER_PEER)] = rows.astype(BF16).reshape(
            C // PER_PEER, PER_PEER, C
        )
        return carry

    lax.fori_loop(0, ROUTE // C, fill_outgoing, 0)

    pl.semaphore_wait(barrier, PEERS - 1)

    own = pltpu.make_async_copy(outgoing.at[me], incoming.at[me], own_sem)
    own.start()

    def push(step, carry):
        dom, tile = peer_of(step, me_dom, me_tile)
        pltpu.make_async_remote_copy(
            src_ref=outgoing.at[dom * 32 + tile],
            dst_ref=incoming.at[me],
            send_sem=send_sem,
            recv_sem=recv_sem,
            device_id=(dom, tile),
            device_id_type=MESH,
        ).start()
        return carry

    lax.fori_loop(0, PEERS - 1, push, 0)

    ahigh, alow = taper_split(ROWS_A, LA, 12.0)
    ohigh, olow = taper_split(ROWS_O, LO, 8.0)
    sub = lax.broadcasted_iota(jnp.int32, (8, M), 0)

    def coeff_block(anom, vec, coeff, t, first):
        rows = vec[pl.ds(first, BLOCK), t, :].astype(BF16)
        halves = [jnp.zeros((8, M), F32)] * 2
        for j in range(BLOCK):
            out = dot_nt(rows, anom[t, first + j])
            half = j // 8
            halves[half] = jnp.where(sub == j % 8, out[half * 8 : half * 8 + 8], halves[half])
        coeff[pl.ds(first, 8), pl.ds(0, M)] = halves[0]
        coeff[pl.ds(first + 8, 8), pl.ds(0, M)] = halves[1]

    def tapered(high, low, coeff):
        value = coeff[...]
        top = value.astype(BF16)
        rest = (value - top.astype(F32)).astype(BF16)
        return dot(high, top) + dot(high, rest) + dot(low, top)

    def halo_copy(side):
        step = 31 if side == 0 else 1
        return pltpu.make_async_remote_copy(
            src_ref=halo_out.at[side],
            dst_ref=halo_in.at[side],
            send_sem=halo_send.at[side],
            recv_sem=halo_recv.at[side],
            device_id=(me_dom, (me_tile + step) % 32),
            device_id_type=MESH,
        )

    for t in range(TD):
        for copy in tile_loads(t):
            copy.wait()

        def atm_block(b, carry, t=t):
            coeff_block(atm, avf, coeff_a, t, b * BLOCK)
            return carry

        def ocn_block(b, carry, t=t):
            coeff_block(ocn, ovf, coeff_o, t, b * BLOCK)
            return carry

        lax.fori_loop(0, LA // BLOCK, atm_block, 0)
        coeff_block(atm, avf, coeff_a, t, LA - BLOCK)
        lax.fori_loop(0, LO // BLOCK, ocn_block, 0)
        coeff_block(ocn, ovf, coeff_o, t, LO - BLOCK)
        wet = sea[t].astype(F32)
        tap_a = tapered(ahigh, alow, coeff_a)
        tap_o = tapered(ohigh, olow, coeff_o) * wet
        vert_a[t] = tap_a
        vert_o[t] = tap_o
        halo_out[t // 2, t % 2, pl.ds(0, ROWS_A), :] = tap_a.astype(BF16)
        halo_out[t // 2, t % 2, pl.ds(ROWS_A, ROWS_O), :] = tap_o.astype(BF16)
        if t % 2 == 1:
            halo_copy(t // 2).start()

    for side in range(2):
        halo_copy(side).wait_recv()

    def neighbour(own, first, rows, index):
        if index < 0:
            return halo_in[1, index + 2, pl.ds(first, rows), :].astype(F32)
        if index >= TD:
            return halo_in[0, index - TD, pl.ds(first, rows), :].astype(F32)
        return own[index]

    def spread(own, codes, first, rows):
        results = []
        for t in range(TD):
            total = jnp.zeros((rows, C), F32)
            for d in range(5):
                total = total + class_weight(codes[t, d]) * neighbour(own, first, rows, t + d - 2)
            results.append(total)
        for t in range(TD):
            own[t] = results[t]

    spread(vert_a, acls, 0, ROWS_A)
    spread(vert_o, ocls, ROWS_A, ROWS_O)

    sub_c = lax.broadcasted_iota(jnp.int32, (8, C), 0)

    def out_block(anom, vert, out, t, first, scale):
        rows = vert[t, pl.ds(first, BLOCK), pl.ds(0, M)].astype(BF16)
        halves = [jnp.zeros((8, C), F32)] * 2
        for j in range(BLOCK):
            value = dot(rows, anom[t, first + j])
            half = j // 8
            halves[half] = jnp.where(sub_c == j % 8, value[half * 8 : half * 8 + 8], halves[half])
        for half in range(2):
            out[pl.ds(first + half * 8, 8), t, :] = halves[half] * scale

    for t in range(TD):
        wet = sea[t].astype(F32)

        def atm_second(b, carry, t=t):
            out_block(atm, vert_a, aout, t, b * BLOCK, 1.0)
            return carry

        def ocn_second(b, carry, t=t, wet=wet):
            out_block(ocn, vert_o, oout, t, b * BLOCK, wet)
            return carry

        lax.fori_loop(0, LA // BLOCK, atm_second, 0)
        out_block(atm, vert_a, aout, t, LA - BLOCK, 1.0)
        lax.fori_loop(0, LO // BLOCK, ocn_second, 0)
        out_block(ocn, vert_o, oout, t, LO - BLOCK, wet)

    own.wait()
    everyone = pltpu.make_async_remote_copy(
        src_ref=outgoing.at[pl.ds(0, PEERS - 1)],
        dst_ref=incoming.at[pl.ds(0, PEERS - 1)],
        send_sem=send_sem,
        recv_sem=recv_sem,
        device_id=(me_dom, (me_tile + 1) % 32),
        device_id_type=MESH,
    )
    everyone.wait_recv()
    arrived = incoming[...].reshape(ROUTE, C)
    for half in range(2):
        cols = pl.ds(half * TD * C, TD * C)
        paired[:, cols] = dot_tn(arrived, recv_map[:, cols])[:M]

    for t in range(TD):
        wet = sea[t].astype(F32)
        own_pair = paired[:, pl.ds(t * C, C)]
        for s in range(KA):
            cross = jnp.sum(atm[t, SURF + s].astype(F32) * own_pair, axis=0, keepdims=True)
            aout[SURF + s, pl.ds(t, 1), :] += cross * (COUPLING * RISE[s])
        own_pair = paired[:, pl.ds((TD + t) * C, C)]
        for o in range(KO):
            cross = jnp.sum(ocn[t, o].astype(F32) * own_pair, axis=0, keepdims=True)
            oout[o, pl.ds(t, 1), :] += cross * (COUPLING * FALL[o]) * wet

    everyone.wait_send()
    for side in range(2):
        halo_copy(side).wait_send()


def local(atm_anom, ocn_anom, atm_vec, ocn_vec, atm_to_ocean, sea_tiles, atm_class, ocn_class):
    hbm = pl.BlockSpec(memory_space=pl.ANY)
    smem = pl.BlockSpec(memory_space=pltpu.SMEM)
    vmem = pl.BlockSpec(memory_space=pltpu.VMEM)
    dma = pltpu.SemaphoreType.DMA
    atm_out, ocn_out = pl.pallas_call(
        kernel,
        out_shape=(
            jax.ShapeDtypeStruct((LA, TD, C), F32),
            jax.ShapeDtypeStruct((LO, TD, C), F32),
        ),
        in_specs=[hbm] * 5 + [smem] * 3,
        out_specs=(vmem, vmem),
        scratch_shapes=[
            pltpu.VMEM((TD, LA, M, C), BF16),
            pltpu.VMEM((TD, LO, M, C), BF16),
            pltpu.VMEM((LA, TD, C), BF16),
            pltpu.VMEM((LO, TD, C), BF16),
            pltpu.VMEM((TD, C), jnp.int32),
            pltpu.VMEM((LA, TD, C), F32),
            pltpu.VMEM((LO, TD, C), F32),
            pltpu.VMEM((ROUTE, 2 * TD * C), BF16),
            pltpu.VMEM((ROUTE, 2 * TD * C), BF16),
            pltpu.VMEM((C, 2 * TD * C), BF16),
            pltpu.VMEM((PEERS, PER_PEER, C), BF16),
            pltpu.VMEM((PEERS, PER_PEER, C), BF16),
            pltpu.VMEM((ROWS_A, C), F32),
            pltpu.VMEM((ROWS_O, C), F32),
            pltpu.VMEM((TD, ROWS_A, C), F32),
            pltpu.VMEM((TD, ROWS_O, C), F32),
            pltpu.VMEM((2, 2, HALO_ROWS, C), BF16),
            pltpu.VMEM((2, 2, HALO_ROWS, C), BF16),
            pltpu.VMEM((M, 2 * TD * C), F32),
            dma((2 + 2 * TD,)),
            dma((3,)),
            dma,
            dma,
            dma,
            dma((2,)),
            dma((2,)),
        ],
        compiler_params=pltpu.CompilerParams(
            collective_id=0, has_side_effects=True, vmem_limit_bytes=40 * 1024 * 1024
        ),
    )(
        jnp.transpose(atm_anom, (0, 2, 1, 3)),
        jnp.transpose(ocn_anom, (0, 2, 1, 3)),
        jnp.transpose(atm_vec, (1, 0, 2)),
        jnp.transpose(ocn_vec, (1, 0, 2)),
        atm_to_ocean,
        sea_tiles,
        atm_class,
        ocn_class,
    )
    return jnp.transpose(atm_out, (1, 0, 2)), jnp.transpose(ocn_out, (1, 0, 2))


def solution(mesh):
    both = ("dom", "tile")
    in_specs = (
        P(both, None, None, None),
        P(both, None, None, None),
        P(both, None, None),
        P(both, None, None),
        P(both, None),
        P(both),
        P(both, None),
        P(both, None),
    )
    out_specs = (P(both, None, None), P(both, None, None))
    return jax.shard_map(local, mesh=mesh, in_specs=in_specs, out_specs=out_specs, check_vma=False)
```

```python
import functools

import jax
import jax.numpy as jnp
import numpy as np
from jax import lax
from jax.experimental import pallas as pl
from jax.experimental.pallas import tpu as pltpu
from jax.sharding import PartitionSpec as P

M = 80
LA = 127
LO = 75
C = 128
KA = 16
KO = 16
TD = 4
BLOCK = 16
SURF = LA - KA
ROWS_A = 128
ROWS_O = 80
HALO_ROWS = ROWS_A + ROWS_O
PEERS = 128
PER_PEER = 8
ROUTE = PEERS * PER_PEER
SLOTS = TD * C
GROUP = 4
UNROLL = 9

COUPLING = 8.0
CLASS_TABLE = (1.0, 0.7, 0.45, 0.25, 0.0)
RISE = [float(np.exp(np.float32(-2.0 * (KA - 1 - s) / KA))) for s in range(KA)]
FALL = [float(np.exp(np.float32(-2.0 * o / KO))) for o in range(KO)]

F32 = jnp.float32
BF16 = jnp.bfloat16
LOGICAL = pl.DeviceIdType.LOGICAL


def class_weight(code):
    weight = jnp.float32(CLASS_TABLE[-1])
    for index in range(len(CLASS_TABLE) - 1):
        weight = jnp.where(code == index, jnp.float32(CLASS_TABLE[index]), weight)
    return weight


def taper_split(rows, levels, spread):
    row = lax.broadcasted_iota(jnp.int32, (rows, rows), 0)
    col = lax.broadcasted_iota(jnp.int32, (rows, rows), 1)
    scaled = (row - col).astype(F32) / spread
    full = jnp.exp(-0.5 * scaled * scaled)
    full = jnp.where((row < levels) & (col < levels), full, 0.0)
    high = full.astype(BF16)
    low = (full - high.astype(F32)).astype(BF16)
    return high, low


def dot(a, b):
    return lax.dot_general(a, b, (((1,), (0,)), ((), ())), preferred_element_type=F32)


def dot_nt(a, b):
    return lax.dot_general(a, b, (((1,), (1,)), ((), ())), preferred_element_type=F32)


def dot_tn(a, b):
    return lax.dot_general(a, b, (((0,), (0,)), ((), ())), preferred_element_type=F32)


def wrap(index, size):
    return jnp.where(index >= size, index - size, index)


def for_peers(me, action):
    def several(step, carry):
        for k in range(UNROLL):
            action(wrap(me + 1 + step * UNROLL + k, PEERS))
        return carry

    lax.fori_loop(0, (PEERS - 1) // UNROLL, several, 0)
    action(wrap(me + PEERS - 1, PEERS))


def lanes_sum(x):
    return jnp.sum(x, axis=1, keepdims=True)


def kernel(
    atm_hbm, ocn_hbm, avec_hbm, ovec_hbm, pair_hbm, sea, acls, ocls, aout, oout,
    atm, ocn, avec, ovec, pairing, avf, ovf, slot_map, proj_a, routed, outgoing, incoming,
    coeff_a, coeff_o, vert_a, vert_o, halo_out, halo_in, paired,
    load_sems, small_sems, send_sem, recv_sem, own_sem, halo_send, halo_recv,
):
    me_dom, me_tile = lax.axis_index("dom"), lax.axis_index("tile")
    me = me_dom * 32 + me_tile

    def small_loads():
        return [
            pltpu.make_async_copy(pair_hbm, pairing, small_sems.at[2]),
            pltpu.make_async_copy(ovec_hbm, ovec, small_sems.at[1]),
            pltpu.make_async_copy(avec_hbm, avec, small_sems.at[0]),
        ]

    def surface_loads():
        return [
            pltpu.make_async_copy(
                ocn_hbm.at[:, pl.ds(0, KO)], ocn.at[:, pl.ds(0, KO)], load_sems.at[0]
            ),
            pltpu.make_async_copy(
                atm_hbm.at[:, pl.ds(SURF, KA)], atm.at[:, pl.ds(SURF, KA)], load_sems.at[1]
            ),
        ]

    def tile_loads(t):
        return [
            pltpu.make_async_copy(
                atm_hbm.at[t, pl.ds(0, SURF)], atm.at[t, pl.ds(0, SURF)], load_sems.at[2 + 2 * t]
            ),
            pltpu.make_async_copy(
                ocn_hbm.at[t, pl.ds(KO, LO - KO)],
                ocn.at[t, pl.ds(KO, LO - KO)],
                load_sems.at[3 + 2 * t],
            ),
        ]

    for copy in small_loads() + surface_loads():
        copy.start()
    for t in range(TD):
        for copy in tile_loads(t):
            copy.start()

    barrier = pltpu.get_barrier_semaphore()

    def greet(peer):
        pl.semaphore_signal(barrier, inc=1, device_id=peer, device_id_type=LOGICAL)

    for_peers(me, greet)

    proj_a[pl.ds(M, C - M), :] = jnp.zeros((C - M, SLOTS), BF16)
    lane = lax.broadcasted_iota(jnp.int32, (1, C), 1)
    lanes = lax.broadcasted_iota(jnp.int32, (M, C), 1)
    sub = lax.broadcasted_iota(jnp.int32, (8, C), 0)

    for copy in small_loads():
        copy.wait()
    avf[...] = avec[...].astype(F32).reshape(LA * TD, C)
    ovf[...] = ovec[...].astype(F32).reshape(LO * TD, C)

    def vector_rows(vec, t, first, count):
        return vec[pl.ds(first * TD + t, count, stride=TD), :]

    for t in range(TD):
        slot = lax.shift_right_logical(pairing[pl.ds(t, 1), :], 7)

        def one_hot(b, carry, t=t, slot=slot):
            start = pl.multiple_of(b * C, C)
            row = lax.broadcasted_iota(jnp.int32, (C, C), 0) + start
            slot_map[pl.ds(start, C), pl.ds(t * C, C)] = jnp.where(row == slot, 1.0, 0.0).astype(
                BF16
            )
            return carry

        lax.fori_loop(0, SLOTS // C, one_hot, 0)

    for copy in surface_loads():
        copy.wait()

    def surface(anom, vec, t, first, scale):
        rows = vector_rows(vec, t, first, KA)
        total = jnp.zeros((M, C), F32)
        found = jnp.zeros((M, C), F32)
        for s in range(KA):
            product = anom[t, first + s].astype(F32) * (rows[s : s + 1] * scale[s])
            total = total + product
            found = jnp.where(lanes == s, lanes_sum(product), found)
        undo = jnp.zeros((1, C), F32)
        for s in range(KA):
            undo = jnp.where(lane == s, 1.0 / scale[s], undo)
        return total, found * undo

    def surface_tile(t, carry):
        wet = sea[t].astype(F32)
        total, found = surface(ocn, ovf, t, 0, FALL)
        coeff_o[t] = found
        turned = jnp.transpose(total * wet)
        routed[pl.ds(TD + t, C, stride=PER_PEER), pl.ds(0, M)] = turned
        total, found = surface(atm, avf, t, SURF, RISE)
        coeff_a[t] = pltpu.roll(found, SURF, 1)
        proj_a[pl.ds(0, M), pl.ds(pl.multiple_of(t * C, C), C)] = total.astype(BF16)
        return carry

    lax.fori_loop(0, TD, surface_tile, 0)

    for b in range(SLOTS // C):
        rows = dot_nt(slot_map[pl.ds(b * C, C), :], proj_a[...])
        for q in range(C // TD):
            routed[pl.ds((b * (C // TD) + q) * PER_PEER, TD), :] = rows[q * TD : q * TD + TD]
    outgoing[...] = routed[...].astype(BF16).reshape(PEERS, PER_PEER, C)

    pl.semaphore_wait(barrier, PEERS - 1)

    own = pltpu.make_async_copy(outgoing.at[me], incoming.at[me], own_sem)
    own.start()

    def push(peer):
        pltpu.make_async_remote_copy(
            src_ref=outgoing.at[peer],
            dst_ref=incoming.at[me],
            send_sem=send_sem,
            recv_sem=recv_sem,
            device_id=peer,
            device_id_type=LOGICAL,
        ).start()

    for_peers(me, push)

    def coeff_block(anom, vec, coeff, t, first):
        rows = vector_rows(vec, t, first, BLOCK)
        spot = lax.broadcasted_iota(jnp.int32, (BLOCK, C), 0)
        left = jnp.where(spot < GROUP, rows, 0.0).astype(BF16)
        right = jnp.where((spot >= GROUP) & (spot < 2 * GROUP), rows, 0.0).astype(BF16)
        stack = jnp.concatenate(
            [
                anom[t, pl.ds(first, GROUP)].reshape(GROUP * M, C),
                anom[t, pl.ds(first + GROUP, GROUP)].reshape(GROUP * M, C),
            ],
            axis=1,
        )
        out = dot_nt(stack, jnp.concatenate([left, right], axis=1))
        out = jnp.concatenate([out, jnp.zeros((GROUP * M, C - BLOCK), F32)], axis=1)
        found = jnp.zeros((M, C), F32)
        for g in range(GROUP):
            found = jnp.where(
                (lanes == g) | (lanes == g + GROUP), out[g * M : (g + 1) * M], found
            )
        for j in range(2 * GROUP, BLOCK):
            product = anom[t, first + j].astype(F32) * rows[j : j + 1]
            found = jnp.where(lanes == j, lanes_sum(product), found)
        moved = pltpu.roll(found, first, 1)
        here = (lanes >= first) & (lanes < first + BLOCK)
        coeff[t] = jnp.where(here, moved, coeff[t])

    ahigh, alow = taper_split(ROWS_A, LA, 12.0)
    ohigh, olow = taper_split(C, LO, 8.0)

    def tapered(high, low, value):
        top = value.astype(BF16)
        rest = (value - top.astype(F32)).astype(BF16)
        return dot_nt(high, top) + dot_nt(high, rest) + dot_nt(low, top)

    def halo_copy(side):
        step = 31 if side == 0 else 1
        return pltpu.make_async_remote_copy(
            src_ref=halo_out.at[side],
            dst_ref=halo_in.at[side],
            send_sem=halo_send.at[side],
            recv_sem=halo_recv.at[side],
            device_id=me_dom * 32 + wrap(me_tile + step, 32),
            device_id_type=LOGICAL,
        )

    def first_pass(t, carry):
        def atm_block(b, inner):
            coeff_block(atm, avf, coeff_a, t, jnp.minimum(b * BLOCK, SURF - BLOCK))
            return inner

        def ocn_block(b, inner):
            coeff_block(ocn, ovf, coeff_o, t, KO + jnp.minimum(b * BLOCK, LO - KO - BLOCK))
            return inner

        lax.fori_loop(0, pl.cdiv(SURF, BLOCK), atm_block, 0)
        lax.fori_loop(0, pl.cdiv(LO - KO, BLOCK), ocn_block, 0)
        wet = sea[t].astype(F32)
        tap_a = tapered(ahigh, alow, coeff_a[t])
        tap_o = tapered(ohigh[:ROWS_O], olow[:ROWS_O], coeff_o[t]) * wet
        vert_a[t] = tap_a
        vert_o[t] = tap_o
        side, place = t // 2, t % 2
        halo_out[side, place, pl.ds(0, ROWS_A), :] = tap_a.astype(BF16)
        halo_out[side, place, pl.ds(ROWS_A, ROWS_O), :] = tap_o.astype(BF16)
        return carry

    for side in range(2):
        for t in (2 * side, 2 * side + 1):
            for copy in tile_loads(t):
                copy.wait()
        lax.fori_loop(2 * side, 2 * side + 2, first_pass, 0)
        halo_copy(side).start()

    own.wait()
    everyone = pltpu.make_async_remote_copy(
        src_ref=outgoing.at[pl.ds(0, PEERS - 1)],
        dst_ref=incoming.at[pl.ds(0, PEERS - 1)],
        send_sem=send_sem,
        recv_sem=recv_sem,
        device_id=me_dom * 32 + wrap(me_tile + 1, 32),
        device_id_type=LOGICAL,
    )
    everyone.wait_recv()
    everyone.wait_send()
    routed[...] = incoming[...].astype(F32).reshape(ROUTE, C)
    for t in range(TD):
        turned = jnp.transpose(routed[pl.ds(t, C, stride=PER_PEER), :])
        paired[:, pl.ds((TD + t) * C, C)] = turned[:M]
    for_atm = jnp.concatenate(
        [routed[pl.ds(q * PER_PEER + TD, TD), :] for q in range(PEERS)], axis=0
    )
    paired[:, pl.ds(0, SLOTS)] = dot_tn(for_atm.astype(BF16), slot_map[...])[:M]

    for side in range(2):
        halo_copy(side).wait_recv()

    def neighbour(own_tiles, first, rows, index):
        if index < 0:
            return halo_in[1, index + 2, pl.ds(first, rows), :].astype(F32)
        if index >= TD:
            return halo_in[0, index - TD, pl.ds(first, rows), :].astype(F32)
        return own_tiles[index]

    def spread(own_tiles, codes, first, rows):
        results = []
        for t in range(TD):
            total = jnp.zeros((rows, M), F32)
            for d in range(5):
                total = total + class_weight(codes[t, d]) * neighbour(
                    own_tiles, first, rows, t + d - 2
                )
            results.append(total)
        for t in range(TD):
            own_tiles[t] = results[t]

    spread(vert_a, acls, 0, ROWS_A)
    spread(vert_o, ocls, ROWS_A, ROWS_O)

    wide = lax.broadcasted_iota(jnp.int32, (BLOCK, BLOCK * M), 1)
    tall = lax.broadcasted_iota(jnp.int32, (BLOCK, BLOCK * M), 0)
    diagonal = (wide >= tall * M) & (wide < tall * M + M)

    def out_block(anom, vert, out, t, first, scale):
        rows = vert[t, pl.ds(first, BLOCK), :]
        wide_rows = jnp.where(diagonal, jnp.concatenate([rows] * BLOCK, axis=1), 0.0)
        value = dot(wide_rows.astype(BF16), anom[t, pl.ds(first, BLOCK)].reshape(BLOCK * M, C))
        out[pl.ds(first, BLOCK), t, :] = value * scale

    for t in range(TD):
        wet = sea[t].astype(F32)

        def atm_second(b, carry, t=t):
            out_block(atm, vert_a, aout, t, jnp.minimum(b * BLOCK, LA - BLOCK), 1.0)
            return carry

        def ocn_second(b, carry, t=t, wet=wet):
            out_block(ocn, vert_o, oout, t, jnp.minimum(b * BLOCK, LO - BLOCK), wet)
            return carry

        lax.fori_loop(0, pl.cdiv(LA, BLOCK), atm_second, 0)
        lax.fori_loop(0, pl.cdiv(LO, BLOCK), ocn_second, 0)

    for t in range(TD):
        wet = sea[t].astype(F32)
        own_pair = paired[:, pl.ds(t * C, C)]
        for s in range(KA):
            cross = jnp.sum(atm[t, SURF + s].astype(F32) * own_pair, axis=0, keepdims=True)
            aout[SURF + s, pl.ds(t, 1), :] += cross * (COUPLING * RISE[s])
        own_pair = paired[:, pl.ds((TD + t) * C, C)]
        for o in range(KO):
            cross = jnp.sum(ocn[t, o].astype(F32) * own_pair, axis=0, keepdims=True)
            oout[o, pl.ds(t, 1), :] += cross * (COUPLING * FALL[o]) * wet

    for side in range(2):
        halo_copy(side).wait_send()


def local(atm_anom, ocn_anom, atm_vec, ocn_vec, atm_to_ocean, sea_tiles, atm_class, ocn_class):
    hbm = pl.BlockSpec(memory_space=pltpu.HBM)
    smem = pl.BlockSpec(memory_space=pltpu.SMEM)
    vmem = pl.BlockSpec(memory_space=pltpu.VMEM)
    dma = pltpu.SemaphoreType.DMA
    atm_out, ocn_out = pl.pallas_call(
        kernel,
        out_shape=(
            jax.ShapeDtypeStruct((LA, TD, C), F32),
            jax.ShapeDtypeStruct((LO, TD, C), F32),
        ),
        in_specs=[hbm] * 5 + [smem] * 3,
        out_specs=(vmem, vmem),
        scratch_shapes=[
            pltpu.VMEM((TD, LA, M, C), BF16),
            pltpu.VMEM((TD, LO, M, C), BF16),
            pltpu.VMEM((LA, TD, C), BF16),
            pltpu.VMEM((LO, TD, C), BF16),
            pltpu.VMEM((TD, C), jnp.int32),
            pltpu.VMEM((LA * TD, C), F32),
            pltpu.VMEM((LO * TD, C), F32),
            pltpu.VMEM((SLOTS, SLOTS), BF16),
            pltpu.VMEM((C, SLOTS), BF16),
            pltpu.VMEM((ROUTE, C), F32),
            pltpu.VMEM((PEERS, PER_PEER, C), BF16),
            pltpu.VMEM((PEERS, PER_PEER, C), BF16),
            pltpu.VMEM((TD, M, C), F32),
            pltpu.VMEM((TD, M, C), F32),
            pltpu.VMEM((TD, ROWS_A, M), F32),
            pltpu.VMEM((TD, ROWS_O, M), F32),
            pltpu.VMEM((2, 2, HALO_ROWS, M), BF16),
            pltpu.VMEM((2, 2, HALO_ROWS, M), BF16),
            pltpu.VMEM((M, 2 * SLOTS), F32),
            dma((2 + 2 * TD,)),
            dma((3,)),
            dma,
            dma,
            dma,
            dma((2,)),
            dma((2,)),
        ],
        compiler_params=pltpu.CompilerParams(
            collective_id=0, has_side_effects=True, vmem_limit_bytes=62 * 1024 * 1024
        ),
    )(
        jnp.transpose(atm_anom, (0, 2, 1, 3)),
        jnp.transpose(ocn_anom, (0, 2, 1, 3)),
        jnp.transpose(atm_vec, (1, 0, 2)),
        jnp.transpose(ocn_vec, (1, 0, 2)),
        atm_to_ocean,
        sea_tiles,
        atm_class,
        ocn_class,
    )
    return jnp.transpose(atm_out, (1, 0, 2)), jnp.transpose(ocn_out, (1, 0, 2))


def solution(mesh):
    both = ("dom", "tile")
    in_specs = (
        P(both, None, None, None),
        P(both, None, None, None),
        P(both, None, None),
        P(both, None, None),
        P(both, None),
        P(both),
        P(both, None),
        P(both, None),
    )
    out_specs = (P(both, None, None), P(both, None, None))
    return jax.shard_map(local, mesh=mesh, in_specs=in_specs, out_specs=out_specs, check_vma=False)
```

```python
import functools

import jax
import jax.numpy as jnp
import numpy as np
from jax import lax
from jax.experimental import pallas as pl
from jax.experimental.pallas import tpu as pltpu
from jax.sharding import PartitionSpec as P

M = 80
LA = 127
LO = 75
C = 128
KA = 16
KO = 16
TD = 4
BLOCK = 16
SURF = LA - KA
ROWS_A = 128
ROWS_O = 80
HALO_ROWS = ROWS_A + ROWS_O
PEERS = 128
PER_PEER = 8
ROUTE = PEERS * PER_PEER
SLOTS = TD * C
HALF = BLOCK // 2
UNROLL = 9
ATM_BLOCKS = (0, 16, 32, 48, 64, 80, SURF - BLOCK)
OCN_BLOCKS = (KO, 32, 48, LO - BLOCK)

COUPLING = 8.0
CLASS_TABLE = (1.0, 0.7, 0.45, 0.25, 0.0)
RISE = [float(np.exp(np.float32(-2.0 * (KA - 1 - s) / KA))) for s in range(KA)]
FALL = [float(np.exp(np.float32(-2.0 * o / KO))) for o in range(KO)]

F32 = jnp.float32
BF16 = jnp.bfloat16
LOGICAL = pl.DeviceIdType.LOGICAL


def class_weight(code):
    weight = jnp.float32(CLASS_TABLE[-1])
    for index in range(len(CLASS_TABLE) - 1):
        weight = jnp.where(code == index, jnp.float32(CLASS_TABLE[index]), weight)
    return weight


def taper_split(rows, levels, spread):
    row = lax.broadcasted_iota(jnp.int32, (rows, rows), 0)
    col = lax.broadcasted_iota(jnp.int32, (rows, rows), 1)
    scaled = (row - col).astype(F32) / spread
    full = jnp.exp(-0.5 * scaled * scaled)
    full = jnp.where((row < levels) & (col < levels), full, 0.0)
    high = full.astype(BF16)
    low = (full - high.astype(F32)).astype(BF16)
    return high, low


def dot(a, b):
    return lax.dot_general(a, b, (((1,), (0,)), ((), ())), preferred_element_type=F32)


def dot_nt(a, b):
    return lax.dot_general(a, b, (((1,), (1,)), ((), ())), preferred_element_type=F32)


def dot_tn(a, b):
    return lax.dot_general(a, b, (((0,), (0,)), ((), ())), preferred_element_type=F32)


def wrap(index, size):
    return jnp.where(index >= size, index - size, index)


def for_peers(me, action):
    def several(step, carry):
        for k in range(UNROLL):
            action(wrap(me + 1 + step * UNROLL + k, PEERS))
        return carry

    lax.fori_loop(0, (PEERS - 1) // UNROLL, several, 0)
    action(wrap(me + PEERS - 1, PEERS))


def kernel(
    atm_hbm, ocn_hbm, avec_hbm, ovec_hbm, pair_hbm, sea, acls, ocls, aout, oout,
    atm, ocn, avec, ovec, pairing, avf, ovf, slot_map, proj_a, routed, outgoing, incoming,
    coeff_a, coeff_o, vert_a, vert_o, halo_out, halo_in, paired,
    load_sems, small_sems, send_sem, recv_sem, own_sem, halo_send, halo_recv,
):
    me_dom, me_tile = lax.axis_index("dom"), lax.axis_index("tile")
    me = me_dom * 32 + me_tile

    def small_loads():
        return [
            pltpu.make_async_copy(pair_hbm, pairing, small_sems.at[2]),
            pltpu.make_async_copy(ovec_hbm, ovec, small_sems.at[1]),
            pltpu.make_async_copy(avec_hbm, avec, small_sems.at[0]),
        ]

    def surface_loads():
        return [
            pltpu.make_async_copy(
                ocn_hbm.at[:, pl.ds(0, KO)], ocn.at[:, pl.ds(0, KO)], load_sems.at[0]
            ),
            pltpu.make_async_copy(
                atm_hbm.at[:, pl.ds(SURF, KA)], atm.at[:, pl.ds(SURF, KA)], load_sems.at[1]
            ),
        ]

    def tile_loads(t):
        return [
            pltpu.make_async_copy(
                atm_hbm.at[t, pl.ds(0, SURF)], atm.at[t, pl.ds(0, SURF)], load_sems.at[2 + 2 * t]
            ),
            pltpu.make_async_copy(
                ocn_hbm.at[t, pl.ds(KO, LO - KO)],
                ocn.at[t, pl.ds(KO, LO - KO)],
                load_sems.at[3 + 2 * t],
            ),
        ]

    for copy in small_loads() + surface_loads():
        copy.start()
    for t in range(TD):
        for copy in tile_loads(t):
            copy.start()

    barrier = pltpu.get_barrier_semaphore()

    def greet(peer):
        pl.semaphore_signal(barrier, inc=1, device_id=peer, device_id_type=LOGICAL)

    for_peers(me, greet)

    proj_a[pl.ds(M, C - M), :] = jnp.zeros((C - M, SLOTS), BF16)
    for t in range(TD):
        coeff_a[t, pl.ds(ROWS_A - 8, 8), :] = jnp.zeros((8, M), F32)
        coeff_o[t, pl.ds(ROWS_O - 8, 8), :] = jnp.zeros((8, M), F32)
    sub_m = lax.broadcasted_iota(jnp.int32, (HALF, M), 0)
    sub_c = lax.broadcasted_iota(jnp.int32, (HALF, C), 0)

    for copy in small_loads():
        copy.wait()
    avf[...] = avec[...].astype(F32).reshape(LA * TD, C)
    ovf[...] = ovec[...].astype(F32).reshape(LO * TD, C)

    def vector_rows(vec, t, first, count):
        return vec[pl.ds(first * TD + t, count, stride=TD), :]

    for t in range(TD):
        slot = lax.shift_right_logical(pairing[pl.ds(t, 1), :], 7)

        def one_hot(b, carry, t=t, slot=slot):
            start = pl.multiple_of(b * C, C)
            row = lax.broadcasted_iota(jnp.int32, (C, C), 0) + start
            slot_map[pl.ds(start, C), pl.ds(t * C, C)] = jnp.where(row == slot, 1.0, 0.0).astype(
                BF16
            )
            return carry

        lax.fori_loop(0, SLOTS // C, one_hot, 0)

    def coeff_block(anom, vec, coeff, t, first):
        rows = vector_rows(vec, t, first, BLOCK)
        none = jnp.zeros((HALF, C), F32)
        left = jnp.concatenate([rows[:HALF], none], axis=0)
        right = jnp.concatenate([none, rows[HALF:]], axis=0)
        both = jnp.concatenate([left, right], axis=1).astype(BF16)
        low = jnp.zeros((HALF, M), F32)
        high = jnp.zeros((HALF, M), F32)
        for j in range(HALF):
            pair = jnp.concatenate([anom[t, first + j], anom[t, first + HALF + j]], axis=1)
            out = dot_nt(both, pair)
            low = jnp.where(sub_m == j, out[:HALF], low)
            high = jnp.where(sub_m == j, out[HALF:], high)
        coeff[t, pl.ds(first, HALF), :] = low
        coeff[t, pl.ds(first + HALF, HALF), :] = high

    for copy in surface_loads():
        copy.wait()

    def project(anom, vec, t, first, scale):
        rows = vector_rows(vec, t, first, KA)
        total = jnp.zeros((M, C), F32)
        for s in range(KA):
            total = total + anom[t, first + s].astype(F32) * (rows[s : s + 1] * scale[s])
        return total

    def surface_tile(t, carry):
        wet = sea[t].astype(F32)
        coeff_block(ocn, ovf, coeff_o, t, 0)
        coeff_block(atm, avf, coeff_a, t, SURF)
        turned = jnp.transpose(project(ocn, ovf, t, 0, FALL) * wet)
        routed[pl.ds(TD + t, C, stride=PER_PEER), pl.ds(0, M)] = turned
        total = project(atm, avf, t, SURF, RISE)
        proj_a[pl.ds(0, M), pl.ds(pl.multiple_of(t * C, C), C)] = total.astype(BF16)
        return carry

    lax.fori_loop(0, TD, surface_tile, 0)

    for b in range(SLOTS // C):
        rows = dot_nt(slot_map[pl.ds(b * C, C), :], proj_a[...])
        for q in range(C // TD):
            routed[pl.ds((b * (C // TD) + q) * PER_PEER, TD), :] = rows[q * TD : q * TD + TD]
    outgoing[...] = routed[...].astype(BF16).reshape(PEERS, PER_PEER, C)

    pl.semaphore_wait(barrier, PEERS - 1)

    own = pltpu.make_async_copy(outgoing.at[me], incoming.at[me], own_sem)
    own.start()

    def push(peer):
        pltpu.make_async_remote_copy(
            src_ref=outgoing.at[peer],
            dst_ref=incoming.at[me],
            send_sem=send_sem,
            recv_sem=recv_sem,
            device_id=peer,
            device_id_type=LOGICAL,
        ).start()

    for_peers(me, push)

    ahigh, alow = taper_split(ROWS_A, LA, 12.0)
    ohigh, olow = taper_split(ROWS_O, LO, 8.0)

    def tapered(high, low, value):
        top = value.astype(BF16)
        rest = (value - top.astype(F32)).astype(BF16)
        return dot(high, top) + dot(high, rest) + dot(low, top)

    def halo_copy(t):
        step = jnp.where(t < TD // 2, 31, 1)
        return pltpu.make_async_remote_copy(
            src_ref=halo_out.at[t],
            dst_ref=halo_in.at[t],
            send_sem=halo_send.at[t],
            recv_sem=halo_recv.at[t],
            device_id=me_dom * 32 + wrap(me_tile + step, 32),
            device_id_type=LOGICAL,
        )

    def first_pass(t, carry):
        for copy in tile_loads(t):
            copy.wait()
        for first in ATM_BLOCKS:
            coeff_block(atm, avf, coeff_a, t, first)
        for first in OCN_BLOCKS:
            coeff_block(ocn, ovf, coeff_o, t, first)
        wet = sea[t].astype(F32)
        tap_a = tapered(ahigh, alow, coeff_a[t])
        tap_o = tapered(ohigh, olow, coeff_o[t]) * wet
        vert_a[t] = tap_a
        vert_o[t] = tap_o
        halo_out[t, pl.ds(0, ROWS_A), pl.ds(0, M)] = tap_a.astype(BF16)
        halo_out[t, pl.ds(ROWS_A, ROWS_O), pl.ds(0, M)] = tap_o.astype(BF16)
        halo_copy(t).start()
        return carry

    lax.fori_loop(0, TD, first_pass, 0)

    own.wait()
    everyone = pltpu.make_async_remote_copy(
        src_ref=outgoing.at[pl.ds(0, PEERS - 1)],
        dst_ref=incoming.at[pl.ds(0, PEERS - 1)],
        send_sem=send_sem,
        recv_sem=recv_sem,
        device_id=me_dom * 32 + wrap(me_tile + 1, 32),
        device_id_type=LOGICAL,
    )
    everyone.wait_recv()
    everyone.wait_send()
    routed[...] = incoming[...].astype(F32).reshape(ROUTE, C)
    for t in range(TD):
        turned = jnp.transpose(routed[pl.ds(t, C, stride=PER_PEER), :])
        paired[:, pl.ds((TD + t) * C, C)] = turned[:M]
    for_atm = jnp.concatenate(
        [routed[pl.ds(q * PER_PEER + TD, TD), :] for q in range(PEERS)], axis=0
    )
    paired[:, pl.ds(0, SLOTS)] = dot_tn(for_atm.astype(BF16), slot_map[...])[:M]

    for t in range(TD):
        halo_copy(t).wait_recv()

    def neighbour(own_tiles, first, rows, index):
        if 0 <= index < TD:
            return own_tiles[index]
        return halo_in[index % TD, pl.ds(first, rows), pl.ds(0, M)].astype(F32)

    def spread(own_tiles, codes, first, rows):
        results = []
        for t in range(TD):
            total = jnp.zeros((rows, M), F32)
            for d in range(5):
                total = total + class_weight(codes[t, d]) * neighbour(
                    own_tiles, first, rows, t + d - 2
                )
            results.append(total)
        for t in range(TD):
            own_tiles[t] = results[t]

    spread(vert_a, acls, 0, ROWS_A)
    spread(vert_o, ocls, ROWS_A, ROWS_O)

    wide = lax.broadcasted_iota(jnp.int32, (BLOCK, BLOCK * M), 1)
    tall = lax.broadcasted_iota(jnp.int32, (BLOCK, BLOCK * M), 0)
    diagonal = (wide >= tall * M) & (wide < tall * M + M)

    def out_block(anom, vert, t, first):
        rows = vert[t, pl.ds(first, BLOCK), :]
        wide_rows = jnp.where(diagonal, jnp.concatenate([rows] * BLOCK, axis=1), 0.0)
        return dot(wide_rows.astype(BF16), anom[t, pl.ds(first, BLOCK)].reshape(BLOCK * M, C))

    def crossed(anom, t, first, pair, scale):
        halves = []
        for half in range(2):
            found = jnp.zeros((HALF, C), F32)
            for s in range(HALF):
                level = half * HALF + s
                cross = jnp.sum(anom[t, first + level].astype(F32) * pair, axis=0, keepdims=True)
                found = jnp.where(sub_c == s, cross * (COUPLING * scale[level]), found)
            halves.append(found)
        return jnp.concatenate(halves, axis=0)

    def second_pass(t, carry):
        wet = sea[t].astype(F32)
        pair = paired[:, pl.ds(pl.multiple_of(t * C, C), C)]
        for first in ATM_BLOCKS[:-1] + (SURF - BLOCK, SURF):
            value = out_block(atm, vert_a, t, first)
            if first == SURF:
                value = value + crossed(atm, t, SURF, pair, RISE)
            aout[pl.ds(first, BLOCK), t, :] = value
        pair = paired[:, pl.ds(pl.multiple_of((TD + t) * C, C), C)]
        for first in (0,) + OCN_BLOCKS:
            value = out_block(ocn, vert_o, t, first)
            if first == 0:
                value = value + crossed(ocn, t, 0, pair, FALL)
            oout[pl.ds(first, BLOCK), t, :] = value * wet
        return carry

    lax.fori_loop(0, TD, second_pass, 0)

    for t in range(TD):
        halo_copy(t).wait_send()


def local(atm_anom, ocn_anom, atm_vec, ocn_vec, atm_to_ocean, sea_tiles, atm_class, ocn_class):
    hbm = pl.BlockSpec(memory_space=pltpu.HBM)
    smem = pl.BlockSpec(memory_space=pltpu.SMEM)
    vmem = pl.BlockSpec(memory_space=pltpu.VMEM)
    dma = pltpu.SemaphoreType.DMA
    atm_out, ocn_out = pl.pallas_call(
        kernel,
        out_shape=(
            jax.ShapeDtypeStruct((LA, TD, C), F32),
            jax.ShapeDtypeStruct((LO, TD, C), F32),
        ),
        in_specs=[hbm] * 5 + [smem] * 3,
        out_specs=(vmem, vmem),
        scratch_shapes=[
            pltpu.VMEM((TD, LA, M, C), BF16),
            pltpu.VMEM((TD, LO, M, C), BF16),
            pltpu.VMEM((LA, TD, C), BF16),
            pltpu.VMEM((LO, TD, C), BF16),
            pltpu.VMEM((TD, C), jnp.int32),
            pltpu.VMEM((LA * TD, C), F32),
            pltpu.VMEM((LO * TD, C), F32),
            pltpu.VMEM((SLOTS, SLOTS), BF16),
            pltpu.VMEM((C, SLOTS), BF16),
            pltpu.VMEM((ROUTE, C), F32),
            pltpu.VMEM((PEERS, PER_PEER, C), BF16),
            pltpu.VMEM((PEERS, PER_PEER, C), BF16),
            pltpu.VMEM((TD, ROWS_A, M), F32),
            pltpu.VMEM((TD, ROWS_O, M), F32),
            pltpu.VMEM((TD, ROWS_A, M), F32),
            pltpu.VMEM((TD, ROWS_O, M), F32),
            pltpu.VMEM((TD, HALO_ROWS, C), BF16),
            pltpu.VMEM((TD, HALO_ROWS, C), BF16),
            pltpu.VMEM((M, 2 * SLOTS), F32),
            dma((2 + 2 * TD,)),
            dma((3,)),
            dma,
            dma,
            dma,
            dma((TD,)),
            dma((TD,)),
        ],
        compiler_params=pltpu.CompilerParams(
            collective_id=0, has_side_effects=True, vmem_limit_bytes=62 * 1024 * 1024
        ),
    )(
        jnp.transpose(atm_anom, (0, 2, 1, 3)),
        jnp.transpose(ocn_anom, (0, 2, 1, 3)),
        jnp.transpose(atm_vec, (1, 0, 2)),
        jnp.transpose(ocn_vec, (1, 0, 2)),
        atm_to_ocean,
        sea_tiles,
        atm_class,
        ocn_class,
    )
    return jnp.transpose(atm_out, (1, 0, 2)), jnp.transpose(ocn_out, (1, 0, 2))


def solution(mesh):
    both = ("dom", "tile")
    in_specs = (
        P(both, None, None, None),
        P(both, None, None, None),
        P(both, None, None),
        P(both, None, None),
        P(both, None),
        P(both),
        P(both, None),
        P(both, None),
    )
    out_specs = (P(both, None, None), P(both, None, None))
    return jax.shard_map(local, mesh=mesh, in_specs=in_specs, out_specs=out_specs, check_vma=False)
```

```python
import functools

import jax
import jax.numpy as jnp
import numpy as np
from jax import lax
from jax.experimental import pallas as pl
from jax.experimental.pallas import tpu as pltpu
from jax.sharding import PartitionSpec as P

M = 80
LA = 127
LO = 75
C = 128
KA = 16
KO = 16
TD = 4
BLOCK = 16
SURF = LA - KA
ROWS_A = 128
ROWS_O = 80
HALO_ROWS = ROWS_A + ROWS_O
PEERS = 128
PER_PEER = 8
ROUTE = PEERS * PER_PEER
SLOTS = TD * C
HALF = BLOCK // 2
UNROLL = 9
ATM_BLOCKS = (0, 16, 32, 48, 64, 80, SURF - BLOCK)
OCN_BLOCKS = (KO, 32, 48, LO - BLOCK)

COUPLING = 8.0
CLASS_TABLE = (1.0, 0.7, 0.45, 0.25, 0.0)
RISE = [float(np.exp(np.float32(-2.0 * (KA - 1 - s) / KA))) for s in range(KA)]
FALL = [float(np.exp(np.float32(-2.0 * o / KO))) for o in range(KO)]

F32 = jnp.float32
BF16 = jnp.bfloat16
LOGICAL = pl.DeviceIdType.LOGICAL


def class_weight(code):
    weight = jnp.float32(CLASS_TABLE[-1])
    for index in range(len(CLASS_TABLE) - 1):
        weight = jnp.where(code == index, jnp.float32(CLASS_TABLE[index]), weight)
    return weight


def taper_split(rows, levels, spread):
    row = lax.broadcasted_iota(jnp.int32, (rows, rows), 0)
    col = lax.broadcasted_iota(jnp.int32, (rows, rows), 1)
    scaled = (row - col).astype(F32) / spread
    full = jnp.exp(-0.5 * scaled * scaled)
    full = jnp.where((row < levels) & (col < levels), full, 0.0)
    high = full.astype(BF16)
    low = (full - high.astype(F32)).astype(BF16)
    return high, low


def dot(a, b):
    return lax.dot_general(a, b, (((1,), (0,)), ((), ())), preferred_element_type=F32)


def dot_nt(a, b):
    return lax.dot_general(a, b, (((1,), (1,)), ((), ())), preferred_element_type=F32)


def dot_tn(a, b):
    return lax.dot_general(a, b, (((0,), (0,)), ((), ())), preferred_element_type=F32)


def wrap(index, size):
    return jnp.where(index >= size, index - size, index)


def for_peers(me, action):
    def several(step, carry):
        for k in range(UNROLL):
            action(wrap(me + 1 + step * UNROLL + k, PEERS))
        return carry

    lax.fori_loop(0, (PEERS - 1) // UNROLL, several, 0)
    action(wrap(me + PEERS - 1, PEERS))


def kernel(
    atm_hbm, ocn_hbm, avec_hbm, ovec_hbm, pair_hbm, sea_hbm, acls_hbm, ocls_hbm, aout, oout,
    atm, ocn, sea, acls, ocls, avec, ovec, pairing, avf, ovf, slot_map, proj_a, routed, outgoing, incoming,
    coeff_a, coeff_o, vert_a, vert_o, halo_out, halo_in, paired,
    load_sems, small_sems, send_sem, recv_sem, own_sem, halo_send, halo_recv,
):
    me_dom, me_tile = lax.axis_index("dom"), lax.axis_index("tile")
    me = me_dom * 32 + me_tile

    def small_loads():
        return [
            pltpu.make_async_copy(pair_hbm, pairing, small_sems.at[2]),
            pltpu.make_async_copy(ovec_hbm, ovec, small_sems.at[1]),
            pltpu.make_async_copy(avec_hbm, avec, small_sems.at[0]),
            pltpu.make_async_copy(sea_hbm, sea, small_sems.at[3]),
            pltpu.make_async_copy(acls_hbm, acls, small_sems.at[4]),
            pltpu.make_async_copy(ocls_hbm, ocls, small_sems.at[5]),
        ]

    def surface_loads():
        return [
            pltpu.make_async_copy(
                ocn_hbm.at[:, pl.ds(0, KO)], ocn.at[:, pl.ds(0, KO)], load_sems.at[0]
            ),
            pltpu.make_async_copy(
                atm_hbm.at[:, pl.ds(SURF, KA)], atm.at[:, pl.ds(SURF, KA)], load_sems.at[1]
            ),
        ]

    def tile_loads(t):
        return [
            pltpu.make_async_copy(
                atm_hbm.at[t, pl.ds(0, SURF)], atm.at[t, pl.ds(0, SURF)], load_sems.at[2 + 2 * t]
            ),
            pltpu.make_async_copy(
                ocn_hbm.at[t, pl.ds(KO, LO - KO)],
                ocn.at[t, pl.ds(KO, LO - KO)],
                load_sems.at[3 + 2 * t],
            ),
        ]

    for copy in small_loads() + surface_loads():
        copy.start()
    for t in range(TD):
        for copy in tile_loads(t):
            copy.start()

    barrier = pltpu.get_barrier_semaphore()

    def greet(peer):
        pl.semaphore_signal(barrier, inc=1, device_id=peer, device_id_type=LOGICAL)

    for_peers(me, greet)

    proj_a[pl.ds(M, C - M), :] = jnp.zeros((C - M, SLOTS), BF16)
    for t in range(TD):
        coeff_a[t, pl.ds(ROWS_A - 8, 8), :] = jnp.zeros((8, M), F32)
        coeff_o[t, pl.ds(ROWS_O - 8, 8), :] = jnp.zeros((8, M), F32)
    sub_m = lax.broadcasted_iota(jnp.int32, (HALF, M), 0)
    sub_c = lax.broadcasted_iota(jnp.int32, (HALF, C), 0)

    for copy in small_loads():
        copy.wait()
    avf[...] = avec[...].astype(F32).reshape(LA * TD, C)
    ovf[...] = ovec[...].astype(F32).reshape(LO * TD, C)

    def vector_rows(vec, t, first, count):
        return vec[pl.ds(first * TD + t, count, stride=TD), :]

    for t in range(TD):
        slot = lax.shift_right_logical(pairing[pl.ds(t, 1), :], 7)

        def one_hot(b, carry, t=t, slot=slot):
            start = pl.multiple_of(b * C, C)
            row = lax.broadcasted_iota(jnp.int32, (C, C), 0) + start
            slot_map[pl.ds(start, C), pl.ds(t * C, C)] = jnp.where(row == slot, 1.0, 0.0).astype(
                BF16
            )
            return carry

        lax.fori_loop(0, SLOTS // C, one_hot, 0)

    def coeff_block(anom, vec, coeff, t, first):
        rows = vector_rows(vec, t, first, BLOCK)
        none = jnp.zeros((HALF, C), F32)
        left = jnp.concatenate([rows[:HALF], none], axis=0)
        right = jnp.concatenate([none, rows[HALF:]], axis=0)
        both = jnp.concatenate([left, right], axis=1).astype(BF16)
        low = jnp.zeros((HALF, M), F32)
        high = jnp.zeros((HALF, M), F32)
        for j in range(HALF):
            pair = jnp.concatenate([anom[t, first + j], anom[t, first + HALF + j]], axis=1)
            out = dot_nt(both, pair)
            low = jnp.where(sub_m == j, out[:HALF], low)
            high = jnp.where(sub_m == j, out[HALF:], high)
        coeff[t, pl.ds(first, HALF), :] = low
        coeff[t, pl.ds(first + HALF, HALF), :] = high

    for copy in surface_loads():
        copy.wait()

    def project(anom, vec, t, first, scale):
        rows = vector_rows(vec, t, first, KA)
        total = jnp.zeros((M, C), F32)
        for s in range(KA):
            total = total + anom[t, first + s].astype(F32) * (rows[s : s + 1] * scale[s])
        return total

    def surface_tile(t, carry):
        wet = sea[t].astype(F32)
        coeff_block(ocn, ovf, coeff_o, t, 0)
        coeff_block(atm, avf, coeff_a, t, SURF)
        turned = jnp.transpose(project(ocn, ovf, t, 0, FALL) * wet)
        routed[pl.ds(TD + t, C, stride=PER_PEER), pl.ds(0, M)] = turned
        total = project(atm, avf, t, SURF, RISE)
        proj_a[pl.ds(0, M), pl.ds(pl.multiple_of(t * C, C), C)] = total.astype(BF16)
        return carry

    lax.fori_loop(0, TD, surface_tile, 0)

    for b in range(SLOTS // C):
        rows = dot_nt(slot_map[pl.ds(b * C, C), :], proj_a[...])
        for q in range(C // TD):
            routed[pl.ds((b * (C // TD) + q) * PER_PEER, TD), :] = rows[q * TD : q * TD + TD]
    outgoing[...] = routed[...].astype(BF16).reshape(PEERS, PER_PEER, C)

    pl.semaphore_wait(barrier, PEERS - 1)

    own = pltpu.make_async_copy(outgoing.at[me], incoming.at[me], own_sem)
    own.start()

    def push(peer):
        pltpu.make_async_remote_copy(
            src_ref=outgoing.at[peer],
            dst_ref=incoming.at[me],
            send_sem=send_sem,
            recv_sem=recv_sem,
            device_id=peer,
            device_id_type=LOGICAL,
        ).start()

    for_peers(me, push)

    ahigh, alow = taper_split(ROWS_A, LA, 12.0)
    ohigh, olow = taper_split(ROWS_O, LO, 8.0)

    def tapered(high, low, value):
        top = value.astype(BF16)
        rest = (value - top.astype(F32)).astype(BF16)
        return dot(high, top) + dot(high, rest) + dot(low, top)

    def halo_copy(t):
        step = jnp.where(t < TD // 2, 31, 1)
        return pltpu.make_async_remote_copy(
            src_ref=halo_out.at[t],
            dst_ref=halo_in.at[t],
            send_sem=halo_send.at[t],
            recv_sem=halo_recv.at[t],
            device_id=me_dom * 32 + wrap(me_tile + step, 32),
            device_id_type=LOGICAL,
        )

    def first_pass(t, carry):
        for copy in tile_loads(t):
            copy.wait()
        for first in ATM_BLOCKS:
            coeff_block(atm, avf, coeff_a, t, first)
        for first in OCN_BLOCKS:
            coeff_block(ocn, ovf, coeff_o, t, first)
        wet = sea[t].astype(F32)
        tap_a = tapered(ahigh, alow, coeff_a[t])
        tap_o = tapered(ohigh, olow, coeff_o[t]) * wet
        vert_a[t] = tap_a
        vert_o[t] = tap_o
        halo_out[t, pl.ds(0, ROWS_A), pl.ds(0, M)] = tap_a.astype(BF16)
        halo_out[t, pl.ds(ROWS_A, ROWS_O), pl.ds(0, M)] = tap_o.astype(BF16)
        halo_copy(t).start()
        return carry

    lax.fori_loop(0, TD, first_pass, 0)

    own.wait()
    everyone = pltpu.make_async_remote_copy(
        src_ref=outgoing.at[pl.ds(0, PEERS - 1)],
        dst_ref=incoming.at[pl.ds(0, PEERS - 1)],
        send_sem=send_sem,
        recv_sem=recv_sem,
        device_id=me_dom * 32 + wrap(me_tile + 1, 32),
        device_id_type=LOGICAL,
    )
    everyone.wait_recv()
    everyone.wait_send()
    routed[...] = incoming[...].astype(F32).reshape(ROUTE, C)
    for t in range(TD):
        turned = jnp.transpose(routed[pl.ds(t, C, stride=PER_PEER), :])
        paired[:, pl.ds((TD + t) * C, C)] = turned[:M]
    for_atm = jnp.concatenate(
        [routed[pl.ds(q * PER_PEER + TD, TD), :] for q in range(PEERS)], axis=0
    )
    paired[:, pl.ds(0, SLOTS)] = dot_tn(for_atm.astype(BF16), slot_map[...])[:M]

    for t in range(TD):
        halo_copy(t).wait_recv()

    def neighbour(own_tiles, first, rows, index):
        if 0 <= index < TD:
            return own_tiles[index]
        return halo_in[index % TD, pl.ds(first, rows), pl.ds(0, M)].astype(F32)

    def spread(own_tiles, codes, first, rows):
        results = []
        for t in range(TD):
            total = jnp.zeros((rows, M), F32)
            for d in range(5):
                total = total + class_weight(codes[t, d]) * neighbour(
                    own_tiles, first, rows, t + d - 2
                )
            results.append(total)
        for t in range(TD):
            own_tiles[t] = results[t]

    spread(vert_a, acls, 0, ROWS_A)
    spread(vert_o, ocls, ROWS_A, ROWS_O)

    wide = lax.broadcasted_iota(jnp.int32, (BLOCK, BLOCK * M), 1)
    tall = lax.broadcasted_iota(jnp.int32, (BLOCK, BLOCK * M), 0)
    diagonal = (wide >= tall * M) & (wide < tall * M + M)

    def out_block(anom, vert, t, first):
        rows = vert[t, pl.ds(first, BLOCK), :]
        wide_rows = jnp.where(diagonal, jnp.concatenate([rows] * BLOCK, axis=1), 0.0)
        return dot(wide_rows.astype(BF16), anom[t, pl.ds(first, BLOCK)].reshape(BLOCK * M, C))

    def crossed(anom, t, first, pair, scale):
        halves = []
        for half in range(2):
            found = jnp.zeros((HALF, C), F32)
            for s in range(HALF):
                level = half * HALF + s
                cross = jnp.sum(anom[t, first + level].astype(F32) * pair, axis=0, keepdims=True)
                found = jnp.where(sub_c == s, cross * (COUPLING * scale[level]), found)
            halves.append(found)
        return jnp.concatenate(halves, axis=0)

    def second_pass(t, carry):
        wet = sea[t].astype(F32)
        pair = paired[:, pl.ds(pl.multiple_of(t * C, C), C)]
        for first in ATM_BLOCKS[:-1] + (SURF - BLOCK, SURF):
            value = out_block(atm, vert_a, t, first)
            if first == SURF:
                value = value + crossed(atm, t, SURF, pair, RISE)
            aout[pl.ds(first, BLOCK), t, :] = value
        pair = paired[:, pl.ds(pl.multiple_of((TD + t) * C, C), C)]
        for first in (0,) + OCN_BLOCKS:
            value = out_block(ocn, vert_o, t, first)
            if first == 0:
                value = value + crossed(ocn, t, 0, pair, FALL)
            oout[pl.ds(first, BLOCK), t, :] = value * wet
        return carry

    lax.fori_loop(0, TD, second_pass, 0)

    for t in range(TD):
        halo_copy(t).wait_send()


def local(atm_anom, ocn_anom, atm_vec, ocn_vec, atm_to_ocean, sea_tiles, atm_class, ocn_class):
    hbm = pl.BlockSpec(memory_space=pltpu.HBM)
    vmem = pl.BlockSpec(memory_space=pltpu.VMEM)
    dma = pltpu.SemaphoreType.DMA
    far = functools.partial(pltpu.with_memory_space_constraint, memory_space=pltpu.HBM)
    atm_out, ocn_out = pl.pallas_call(
        kernel,
        out_shape=(
            jax.ShapeDtypeStruct((LA, TD, C), F32),
            jax.ShapeDtypeStruct((LO, TD, C), F32),
        ),
        in_specs=[hbm] * 8,
        out_specs=(vmem, vmem),
        scratch_shapes=[
            pltpu.VMEM((TD, LA, M, C), BF16),
            pltpu.VMEM((TD, LO, M, C), BF16),
            pltpu.SMEM((TD,), jnp.int32),
            pltpu.SMEM((TD, 5), jnp.int32),
            pltpu.SMEM((TD, 5), jnp.int32),
            pltpu.VMEM((LA, TD, C), BF16),
            pltpu.VMEM((LO, TD, C), BF16),
            pltpu.VMEM((TD, C), jnp.int32),
            pltpu.VMEM((LA * TD, C), F32),
            pltpu.VMEM((LO * TD, C), F32),
            pltpu.VMEM((SLOTS, SLOTS), BF16),
            pltpu.VMEM((C, SLOTS), BF16),
            pltpu.VMEM((ROUTE, C), F32),
            pltpu.VMEM((PEERS, PER_PEER, C), BF16),
            pltpu.VMEM((PEERS, PER_PEER, C), BF16),
            pltpu.VMEM((TD, ROWS_A, M), F32),
            pltpu.VMEM((TD, ROWS_O, M), F32),
            pltpu.VMEM((TD, ROWS_A, M), F32),
            pltpu.VMEM((TD, ROWS_O, M), F32),
            pltpu.VMEM((TD, HALO_ROWS, C), BF16),
            pltpu.VMEM((TD, HALO_ROWS, C), BF16),
            pltpu.VMEM((M, 2 * SLOTS), F32),
            dma((2 + 2 * TD,)),
            dma((6,)),
            dma,
            dma,
            dma,
            dma((TD,)),
            dma((TD,)),
        ],
        compiler_params=pltpu.CompilerParams(
            collective_id=0, has_side_effects=True, vmem_limit_bytes=40 * 1024 * 1024
        ),
    )(
        far(jnp.transpose(atm_anom, (0, 2, 1, 3))),
        far(jnp.transpose(ocn_anom, (0, 2, 1, 3))),
        far(jnp.transpose(atm_vec, (1, 0, 2))),
        far(jnp.transpose(ocn_vec, (1, 0, 2))),
        far(atm_to_ocean),
        far(sea_tiles),
        far(atm_class),
        far(ocn_class),
    )
    return jnp.transpose(atm_out, (1, 0, 2)), jnp.transpose(ocn_out, (1, 0, 2))


def solution(mesh):
    both = ("dom", "tile")
    in_specs = (
        P(both, None, None, None),
        P(both, None, None, None),
        P(both, None, None),
        P(both, None, None),
        P(both, None),
        P(both),
        P(both, None),
        P(both, None),
    )
    out_specs = (P(both, None, None), P(both, None, None))
    return jax.shard_map(local, mesh=mesh, in_specs=in_specs, out_specs=out_specs, check_vma=False)
```

```python
import functools

import jax
import jax.numpy as jnp
import numpy as np
from jax import lax
from jax.experimental import pallas as pl
from jax.experimental.pallas import tpu as pltpu
from jax.sharding import PartitionSpec as P

M = 80
LA = 127
LO = 75
C = 128
KA = 16
KO = 16
TD = 4
BLOCK = 16
SURF = LA - KA
ROWS_A = 128
ROWS_O = 80
HALO_ROWS = ROWS_A + ROWS_O
PEERS = 128
PER_PEER = 8
ROUTE = PEERS * PER_PEER
SLOTS = TD * C
HALF = BLOCK // 2
UNROLL = 9
ATM_BLOCKS = (0, 16, 32, 48, 64, 80, SURF - BLOCK)
OCN_BLOCKS = (KO, 32, 48, LO - BLOCK)

COUPLING = 8.0
CLASS_TABLE = (1.0, 0.7, 0.45, 0.25, 0.0)
RISE = [float(np.exp(np.float32(-2.0 * (KA - 1 - s) / KA))) for s in range(KA)]
FALL = [float(np.exp(np.float32(-2.0 * o / KO))) for o in range(KO)]

F32 = jnp.float32
BF16 = jnp.bfloat16
LOGICAL = pl.DeviceIdType.LOGICAL


def class_weight(code):
    weight = jnp.float32(CLASS_TABLE[-1])
    for index in range(len(CLASS_TABLE) - 1):
        weight = jnp.where(code == index, jnp.float32(CLASS_TABLE[index]), weight)
    return weight


def taper_split(rows, levels, spread):
    row = lax.broadcasted_iota(jnp.int32, (rows, rows), 0)
    col = lax.broadcasted_iota(jnp.int32, (rows, rows), 1)
    scaled = (row - col).astype(F32) / spread
    full = jnp.exp(-0.5 * scaled * scaled)
    full = jnp.where((row < levels) & (col < levels), full, 0.0)
    high = full.astype(BF16)
    low = (full - high.astype(F32)).astype(BF16)
    return high, low


def dot(a, b):
    return lax.dot_general(a, b, (((1,), (0,)), ((), ())), preferred_element_type=F32)


def dot_nt(a, b):
    return lax.dot_general(a, b, (((1,), (1,)), ((), ())), preferred_element_type=F32)


def dot_tn(a, b):
    return lax.dot_general(a, b, (((0,), (0,)), ((), ())), preferred_element_type=F32)


def wrap(index, size):
    return jnp.where(index >= size, index - size, index)


def for_peers(me, action):
    def several(step, carry):
        for k in range(UNROLL):
            action(wrap(me + 1 + step * UNROLL + k, PEERS))
        return carry

    lax.fori_loop(0, (PEERS - 1) // UNROLL, several, 0)
    action(wrap(me + PEERS - 1, PEERS))


def kernel(
    atm_hbm, ocn_hbm, avec_hbm, ovec_hbm, pair_hbm, sea_hbm, acls_hbm, ocls_hbm, aout, oout,
    atm, ocn, sea, acls, ocls, avec, ovec, pairing, avf, ovf, slot_map, proj_a, routed, outgoing, incoming,
    coeff_a, coeff_o, vert_a, vert_o, halo_out, halo_in, paired, cross_a, cross_o,
    load_sems, small_sems, send_sem, recv_sem, own_sem, halo_send, halo_recv,
):
    me_dom, me_tile = lax.axis_index("dom"), lax.axis_index("tile")
    me = me_dom * 32 + me_tile

    def small_loads():
        return [
            pltpu.make_async_copy(pair_hbm, pairing, small_sems.at[2]),
            pltpu.make_async_copy(ovec_hbm, ovec, small_sems.at[1]),
            pltpu.make_async_copy(avec_hbm, avec, small_sems.at[0]),
            pltpu.make_async_copy(sea_hbm, sea, small_sems.at[3]),
            pltpu.make_async_copy(acls_hbm, acls, small_sems.at[4]),
            pltpu.make_async_copy(ocls_hbm, ocls, small_sems.at[5]),
        ]

    def surface_loads():
        return [
            pltpu.make_async_copy(
                ocn_hbm.at[:, pl.ds(0, KO)], ocn.at[:, pl.ds(0, KO)], load_sems.at[0]
            ),
            pltpu.make_async_copy(
                atm_hbm.at[:, pl.ds(SURF, KA)], atm.at[:, pl.ds(SURF, KA)], load_sems.at[1]
            ),
        ]

    def tile_loads(t):
        return [
            pltpu.make_async_copy(
                atm_hbm.at[t, pl.ds(0, SURF)], atm.at[t, pl.ds(0, SURF)], load_sems.at[2 + 2 * t]
            ),
            pltpu.make_async_copy(
                ocn_hbm.at[t, pl.ds(KO, LO - KO)],
                ocn.at[t, pl.ds(KO, LO - KO)],
                load_sems.at[3 + 2 * t],
            ),
        ]

    for copy in small_loads() + surface_loads():
        copy.start()

    barrier = pltpu.get_barrier_semaphore()

    def greet(peer):
        pl.semaphore_signal(barrier, inc=1, device_id=peer, device_id_type=LOGICAL)

    for_peers(me, greet)
    for copy in tile_loads(0):
        copy.start()

    proj_a[pl.ds(M, C - M), :] = jnp.zeros((C - M, SLOTS), BF16)
    for t in range(TD):
        coeff_a[t, pl.ds(ROWS_A - 8, 8), :] = jnp.zeros((8, M), F32)
        coeff_o[t, pl.ds(ROWS_O - 8, 8), :] = jnp.zeros((8, M), F32)
    sub_m = lax.broadcasted_iota(jnp.int32, (HALF, M), 0)
    sub_c = lax.broadcasted_iota(jnp.int32, (HALF, C), 0)

    for copy in small_loads():
        copy.wait()
    avf[...] = avec[...].astype(F32).reshape(LA * TD, C)
    ovf[...] = ovec[...].astype(F32).reshape(LO * TD, C)

    def vector_rows(vec, t, first, count):
        return vec[pl.ds(first * TD + t, count, stride=TD), :]

    for t in range(TD):
        slot = lax.shift_right_logical(pairing[pl.ds(t, 1), :], 7)

        def one_hot(b, carry, t=t, slot=slot):
            start = pl.multiple_of(b * C, C)
            row = lax.broadcasted_iota(jnp.int32, (C, C), 0) + start
            slot_map[pl.ds(start, C), pl.ds(t * C, C)] = jnp.where(row == slot, 1.0, 0.0).astype(
                BF16
            )
            return carry

        lax.fori_loop(0, SLOTS // C, one_hot, 0)

    def coeff_block(anom, vec, coeff, t, first):
        rows = vector_rows(vec, t, first, BLOCK)
        none = jnp.zeros((HALF, C), F32)
        left = jnp.concatenate([rows[:HALF], none], axis=0)
        right = jnp.concatenate([none, rows[HALF:]], axis=0)
        both = jnp.concatenate([left, right], axis=1).astype(BF16)
        low = jnp.zeros((HALF, M), F32)
        high = jnp.zeros((HALF, M), F32)
        for j in range(HALF):
            pair = jnp.concatenate([anom[t, first + j], anom[t, first + HALF + j]], axis=1)
            out = dot_nt(both, pair)
            low = jnp.where(sub_m == j, out[:HALF], low)
            high = jnp.where(sub_m == j, out[HALF:], high)
        coeff[t, pl.ds(first, HALF), :] = low
        coeff[t, pl.ds(first + HALF, HALF), :] = high

    for copy in surface_loads():
        copy.wait()
    for copy in tile_loads(1):
        copy.start()

    def project(anom, vec, t, first, scale):
        rows = vector_rows(vec, t, first, KA)
        total = jnp.zeros((M, C), F32)
        for s in range(KA):
            total = total + anom[t, first + s].astype(F32) * (rows[s : s + 1] * scale[s])
        return total

    def surface_tile(t, carry):
        wet = sea[t].astype(F32)
        coeff_block(ocn, ovf, coeff_o, t, 0)
        coeff_block(atm, avf, coeff_a, t, SURF)
        turned = jnp.transpose(project(ocn, ovf, t, 0, FALL) * wet)
        routed[pl.ds(TD + t, C, stride=PER_PEER), pl.ds(0, M)] = turned
        total = project(atm, avf, t, SURF, RISE)
        proj_a[pl.ds(0, M), pl.ds(pl.multiple_of(t * C, C), C)] = total.astype(BF16)
        return carry

    lax.fori_loop(0, TD, surface_tile, 0)

    for b in range(SLOTS // C):
        rows = dot_nt(slot_map[pl.ds(b * C, C), :], proj_a[...])
        for q in range(C // TD):
            routed[pl.ds((b * (C // TD) + q) * PER_PEER, TD), :] = rows[q * TD : q * TD + TD]
    outgoing[...] = routed[...].astype(BF16).reshape(PEERS, PER_PEER, C)

    pl.semaphore_wait(barrier, PEERS - 1)

    own = pltpu.make_async_copy(outgoing.at[me], incoming.at[me], own_sem)
    own.start()

    def push(peer):
        pltpu.make_async_remote_copy(
            src_ref=outgoing.at[peer],
            dst_ref=incoming.at[me],
            send_sem=send_sem,
            recv_sem=recv_sem,
            device_id=peer,
            device_id_type=LOGICAL,
        ).start()

    for_peers(me, push)

    ahigh, alow = taper_split(ROWS_A, LA, 12.0)
    ohigh, olow = taper_split(ROWS_O, LO, 8.0)

    def tapered(high, low, value):
        top = value.astype(BF16)
        rest = (value - top.astype(F32)).astype(BF16)
        return dot(high, top) + dot(high, rest) + dot(low, top)

    def halo_copy(t):
        step = jnp.where(t < TD // 2, 31, 1)
        return pltpu.make_async_remote_copy(
            src_ref=halo_out.at[t],
            dst_ref=halo_in.at[t],
            send_sem=halo_send.at[t],
            recv_sem=halo_recv.at[t],
            device_id=me_dom * 32 + wrap(me_tile + step, 32),
            device_id_type=LOGICAL,
        )

    def first_pass(t, carry):
        for copy in tile_loads(t):
            copy.wait()

        @pl.when(t < TD - 2)
        def _():
            for copy in tile_loads(t + 2):
                copy.start()

        for first in ATM_BLOCKS:
            coeff_block(atm, avf, coeff_a, t, first)
        for first in OCN_BLOCKS:
            coeff_block(ocn, ovf, coeff_o, t, first)
        wet = sea[t].astype(F32)
        tap_a = tapered(ahigh, alow, coeff_a[t])
        tap_o = tapered(ohigh, olow, coeff_o[t]) * wet
        vert_a[t] = tap_a
        vert_o[t] = tap_o
        halo_out[t, pl.ds(0, ROWS_A), pl.ds(0, M)] = tap_a.astype(BF16)
        halo_out[t, pl.ds(ROWS_A, ROWS_O), pl.ds(0, M)] = tap_o.astype(BF16)
        halo_copy(t).start()
        return carry

    lax.fori_loop(0, TD, first_pass, 0)

    own.wait()
    everyone = pltpu.make_async_remote_copy(
        src_ref=outgoing.at[pl.ds(0, PEERS - 1)],
        dst_ref=incoming.at[pl.ds(0, PEERS - 1)],
        send_sem=send_sem,
        recv_sem=recv_sem,
        device_id=me_dom * 32 + wrap(me_tile + 1, 32),
        device_id_type=LOGICAL,
    )
    everyone.wait_recv()
    everyone.wait_send()
    routed[...] = incoming[...].astype(F32).reshape(ROUTE, C)
    for t in range(TD):
        turned = jnp.transpose(routed[pl.ds(t, C, stride=PER_PEER), :])
        paired[:, pl.ds((TD + t) * C, C)] = turned[:M]
    for_atm = jnp.concatenate(
        [routed[pl.ds(q * PER_PEER + TD, TD), :] for q in range(PEERS)], axis=0
    )
    paired[:, pl.ds(0, SLOTS)] = dot_tn(for_atm.astype(BF16), slot_map[...])[:M]

    def crossed(anom, t, first, pair, scale):
        halves = []
        for half in range(2):
            found = jnp.zeros((HALF, C), F32)
            for s in range(HALF):
                level = half * HALF + s
                cross = jnp.sum(anom[t, first + level].astype(F32) * pair, axis=0, keepdims=True)
                found = jnp.where(sub_c == s, cross * (COUPLING * scale[level]), found)
            halves.append(found)
        return jnp.concatenate(halves, axis=0)

    def cross_tile(t, carry):
        cols = pl.ds(pl.multiple_of(t * C, C), C)
        cross_a[t] = crossed(atm, t, SURF, paired[:, cols], RISE)
        cols = pl.ds(pl.multiple_of((TD + t) * C, C), C)
        cross_o[t] = crossed(ocn, t, 0, paired[:, cols], FALL)
        return carry

    lax.fori_loop(0, TD, cross_tile, 0)

    for t in range(TD):
        halo_copy(t).wait_recv()

    def neighbour(own_tiles, first, rows, index):
        if 0 <= index < TD:
            return own_tiles[index]
        return halo_in[index % TD, pl.ds(first, rows), pl.ds(0, M)].astype(F32)

    def spread(own_tiles, codes, first, rows):
        results = []
        for t in range(TD):
            total = jnp.zeros((rows, M), F32)
            for d in range(5):
                total = total + class_weight(codes[t, d]) * neighbour(
                    own_tiles, first, rows, t + d - 2
                )
            results.append(total)
        for t in range(TD):
            own_tiles[t] = results[t]

    spread(vert_a, acls, 0, ROWS_A)
    spread(vert_o, ocls, ROWS_A, ROWS_O)

    wide = lax.broadcasted_iota(jnp.int32, (BLOCK, BLOCK * M), 1)
    tall = lax.broadcasted_iota(jnp.int32, (BLOCK, BLOCK * M), 0)
    diagonal = (wide >= tall * M) & (wide < tall * M + M)

    def out_block(anom, vert, t, first):
        rows = vert[t, pl.ds(first, BLOCK), :]
        wide_rows = jnp.where(diagonal, jnp.concatenate([rows] * BLOCK, axis=1), 0.0)
        return dot(wide_rows.astype(BF16), anom[t, pl.ds(first, BLOCK)].reshape(BLOCK * M, C))

    def second_pass(t, carry):
        wet = sea[t].astype(F32)
        for first in ATM_BLOCKS[:-1] + (SURF - BLOCK, SURF):
            value = out_block(atm, vert_a, t, first)
            if first == SURF:
                value = value + cross_a[t]
            aout[pl.ds(first, BLOCK), t, :] = value
        for first in (0,) + OCN_BLOCKS:
            value = out_block(ocn, vert_o, t, first)
            if first == 0:
                value = value + cross_o[t]
            oout[pl.ds(first, BLOCK), t, :] = value * wet
        return carry

    lax.fori_loop(0, TD, second_pass, 0)

    for t in range(TD):
        halo_copy(t).wait_send()


def local(atm_anom, ocn_anom, atm_vec, ocn_vec, atm_to_ocean, sea_tiles, atm_class, ocn_class):
    hbm = pl.BlockSpec(memory_space=pltpu.HBM)
    vmem = pl.BlockSpec(memory_space=pltpu.VMEM)
    dma = pltpu.SemaphoreType.DMA
    far = functools.partial(pltpu.with_memory_space_constraint, memory_space=pltpu.HBM)
    atm_out, ocn_out = pl.pallas_call(
        kernel,
        out_shape=(
            jax.ShapeDtypeStruct((LA, TD, C), F32),
            jax.ShapeDtypeStruct((LO, TD, C), F32),
        ),
        in_specs=[hbm] * 8,
        out_specs=(vmem, vmem),
        scratch_shapes=[
            pltpu.VMEM((TD, LA, M, C), BF16),
            pltpu.VMEM((TD, LO, M, C), BF16),
            pltpu.SMEM((TD,), jnp.int32),
            pltpu.SMEM((TD, 5), jnp.int32),
            pltpu.SMEM((TD, 5), jnp.int32),
            pltpu.VMEM((LA, TD, C), BF16),
            pltpu.VMEM((LO, TD, C), BF16),
            pltpu.VMEM((TD, C), jnp.int32),
            pltpu.VMEM((LA * TD, C), F32),
            pltpu.VMEM((LO * TD, C), F32),
            pltpu.VMEM((SLOTS, SLOTS), BF16),
            pltpu.VMEM((C, SLOTS), BF16),
            pltpu.VMEM((ROUTE, C), F32),
            pltpu.VMEM((PEERS, PER_PEER, C), BF16),
            pltpu.VMEM((PEERS, PER_PEER, C), BF16),
            pltpu.VMEM((TD, ROWS_A, M), F32),
            pltpu.VMEM((TD, ROWS_O, M), F32),
            pltpu.VMEM((TD, ROWS_A, M), F32),
            pltpu.VMEM((TD, ROWS_O, M), F32),
            pltpu.VMEM((TD, HALO_ROWS, C), BF16),
            pltpu.VMEM((TD, HALO_ROWS, C), BF16),
            pltpu.VMEM((M, 2 * SLOTS), F32),
            pltpu.VMEM((TD, BLOCK, C), F32),
            pltpu.VMEM((TD, BLOCK, C), F32),
            dma((2 + 2 * TD,)),
            dma((6,)),
            dma,
            dma,
            dma,
            dma((TD,)),
            dma((TD,)),
        ],
        compiler_params=pltpu.CompilerParams(
            collective_id=0, has_side_effects=True, vmem_limit_bytes=40 * 1024 * 1024
        ),
    )(
        far(jnp.transpose(atm_anom, (0, 2, 1, 3))),
        far(jnp.transpose(ocn_anom, (0, 2, 1, 3))),
        far(jnp.transpose(atm_vec, (1, 0, 2))),
        far(jnp.transpose(ocn_vec, (1, 0, 2))),
        far(atm_to_ocean),
        far(sea_tiles),
        far(atm_class),
        far(ocn_class),
    )
    return jnp.transpose(atm_out, (1, 0, 2)), jnp.transpose(ocn_out, (1, 0, 2))


def solution(mesh):
    both = ("dom", "tile")
    in_specs = (
        P(both, None, None, None),
        P(both, None, None, None),
        P(both, None, None),
        P(both, None, None),
        P(both, None),
        P(both),
        P(both, None),
        P(both, None),
    )
    out_specs = (P(both, None, None), P(both, None, None))
    return jax.shard_map(local, mesh=mesh, in_specs=in_specs, out_specs=out_specs, check_vma=False)
```
